256 devices in a mesh: dp: 2 (over core), expert: 128 (over y, x, z).
Axes of the slice: x: 4, y: 4, z: 8, core: 2. Of those that a mesh axis runs over, the one named last changes fastest.
Arguments:
- tokens: bfloat16 [32768, 2048], P(('dp', 'expert')), parts along dimension 0, may hold values from -6 to 6
- cotangent: bfloat16 [32768, 2048], P(('dp', 'expert')), parts along dimension 0, may hold values from -6 to 6
- expert_ids: int32 [32768, 10], P(('dp', 'expert')), parts along dimension 0, may hold values from 0 to 255, all different within a row; in each aligned block of 128 rows (0 to 127, 128 to 255, ...) at most 6 rows name the same one
- probs: float32 [32768, 10], P(('dp', 'expert')), parts along dimension 0, may hold values from 0.05 to 0.5
- gate_weight: bfloat16 [512, 2048, 256], P(('dp', 'expert')), parts along dimension 0, may hold values from -0.125 to 0.125
- up_weight: bfloat16 [512, 2048, 256], P(('dp', 'expert')), parts along dimension 0, may hold values from -0.125 to 0.125
- down_weight: bfloat16 [512, 256, 2048], P(('dp', 'expert')), parts along dimension 0, may hold values from -0.375 to 0.375
Outputs:
- mixed: float32 [32768, 2048], P(('dp', 'expert')), parts along dimension 0
- input_grad: float32 [32768, 2048], P(('dp', 'expert')), parts along dimension 0
The draws below stay inside these ranges and needn't reach their ends.
There are 2 independent parts, one for each index of `dp`. The reference program is written for one: setup_inputs(seed, part) draws one part's arguments, and reference() takes and returns one part's arrays. A program takes and returns all parts, laid end to end along the dimension named above; each array names one. Nothing has to cross between parts.
Inputs may be any that keep to these rules, and one draw needn't show every extreme that they name: `expert_ids`: each row names 10 different experts. Within the 128 rows of one device no expert is named by more than 6 rows, and in some of these blocks one expert is named by exactly 6 rows; loads across experts are skewed.
All inputs are finite; a program needn't handle non-finite values.
Results may differ from the reference program's by a relative error of at most 0.0041.
Values may be sent and summed in bfloat16 or wider, within the bound.
A program may use at most 128 MiB of HBM per device.

```python
import math
import jax
import jax.numpy as jnp
import numpy as np
from jax import lax

D = 2048
H = 256
TOP_K = 10
TOK_DEV = 128
EXPERTS = 256
TOKENS = 16384
CAP = 6
N_EXPERT = 128


def steps_of(own_key, shape, split, low, top_value):
    def one(axis_at, blocks):
        steps = jax.random.uniform(jax.random.fold_in(jax.random.fold_in(own_key, 6), axis_at), (blocks,), jnp.float32, low / len(split), top_value / len(split))
        return jnp.repeat(jnp.exp(steps), shape[axis_at] // blocks).reshape((-1,) + (1,) * (len(shape) - axis_at - 1))

    loudness = one(*split[0])
    for cut in split[1:]:
        loudness = loudness * one(*cut)
    return loudness


def deal_out(stream_key, own, number, rows, amount, top, reach, lean):
    order = jax.random.permutation(stream_key, amount)
    packed, ordinary = shares(amount, rows * top, reach, lean, True), shares(amount, rows * top, reach, lean, False)
    places = jnp.arange(amount)

    def named(lengths, offset_by):
        used = int((lengths > 0).sum())
        fixed = max(1, used // 4)
        passed = fixed + (places - fixed + offset_by * (used - fixed)) % max(1, amount - fixed)
        return jnp.zeros((amount,), jnp.int32).at[order[jnp.where(places < fixed, places, passed)]].set(jnp.asarray(lengths, jnp.int32))

    lengths = jnp.where(number % 4 == 0, named(packed, number // 4), named(ordinary, number - number // 4 - 1))
    mixed = jax.random.permutation(jax.random.fold_in(own, 3), amount)
    giver, taker = mixed[0:amount // 2 * 2:2], mixed[1:amount // 2 * 2:2]
    room = jnp.minimum(lengths[giver] - 1, reach - lengths[taker]) // 2
    room = jnp.where((giver == order[0]) | (taker == order[0]) | (lengths[taker] == 0), 0, jnp.maximum(room, 0))
    passed = jax.random.randint(jax.random.fold_in(own, 4), (amount // 2,), 0, 1 << 20) % (room + 1)
    lengths = lengths.at[giver].add(-passed).at[taker].add(passed)
    members = jnp.searchsorted(jnp.cumsum(lengths), jnp.arange(rows * top), side="right").astype(jnp.int32)
    grid = members.reshape(top, rows).T
    grid = grid[jax.random.permutation(jax.random.fold_in(own, 1), rows)]
    offset_by = jax.random.randint(jax.random.fold_in(own, 2), (rows, 1), 0, top)
    return jnp.take_along_axis(grid, (jnp.arange(top)[None, :] + offset_by) % top, axis=1)


def shares(amount, total, reach, skew, full):
    loads = [(1 << 20) // math.isqrt(standing ** skew) + 1 for standing in range(1, amount + 1)]
    largest = reach if full else min(reach, max(-(-total // amount), total * loads[0] // sum(loads)))
    least = 1 if total - largest >= amount - 1 else 0
    given, surplus = [largest] + [least] * (amount - 1), total - largest - least * (amount - 1)
    while surplus > 0:
        candidates = [i for i in range(1, amount) if given[i] < largest] or [i for i in range(1, amount) if given[i] < reach]
        whole, left = sum([loads[i] for i in candidates]), surplus
        for i in candidates:
            more = min(reach - given[i], max(1, left * loads[i] // whole), surplus)
            given[i] = given[i] + more
            surplus = surplus - more
    return np.array(given)


def normal_values(stream_key, dims, width, reach, cuts=(), kind=jnp.bfloat16):
    entries = jax.random.normal(stream_key, dims, jnp.float32) * width
    if len(cuts) > 0:
        entries = steps_of(stream_key, dims, cuts, -0.22, 0.18) * entries
    return jnp.clip(entries, min=-reach, max=reach).astype(kind)


def setup_inputs(seed: int = 0, part: int = 0) -> dict:
    keys = jax.random.split(jax.random.key(seed), 8)
    part_keys = jax.random.split(jax.random.fold_in(keys[7], part), 8)
    tokens = normal_values(part_keys[0], (TOKENS, D), 1.0, 6.0, ((0, 128),))
    cotangent = normal_values(part_keys[1], (TOKENS, D), 1.0, 6.0, ((0, 128),))
    expert_ids_keys = jax.random.split(jax.random.fold_in(part_keys[2], 1), TOKENS // TOK_DEV)
    expert_ids_turns = jax.random.permutation(jax.random.fold_in(part_keys[2], 3), TOKENS // TOK_DEV)
    expert_ids = jax.vmap(lambda own, number: deal_out(jax.random.fold_in(part_keys[2], 2), own, number, TOK_DEV, EXPERTS, TOP_K, CAP, 2))(expert_ids_keys, expert_ids_turns).reshape((TOKENS, TOP_K))
    probs = jnp.clip(jnp.exp(math.log(0.5) - 2.3025851 * jax.random.uniform(part_keys[3], (TOKENS, TOP_K), jnp.float32) ** steps_of(part_keys[3], (TOKENS, TOP_K), ((0, 128),), -0.2, 0.2)), 0.05, 0.5)
    gate_weight = normal_values(part_keys[4], (EXPERTS, D, H), D ** -0.5, 0.125, ((0, 128),))
    up_weight = normal_values(part_keys[5], (EXPERTS, D, H), D ** -0.5, 0.125, ((0, 128),))
    down_weight = normal_values(part_keys[6], (EXPERTS, H, D), H ** -0.5, 0.375, ((0, 128),))
    return {"tokens": tokens, "cotangent": cotangent, "expert_ids": expert_ids, "probs": probs, "gate_weight": gate_weight, "up_weight": up_weight, "down_weight": down_weight}


def expert_pass(row_block, grad_block, w_gate, w_up, w_down):
    gate_pre = jnp.dot(row_block, w_gate, preferred_element_type=jnp.float32)
    up_pre = jnp.dot(row_block, w_up, preferred_element_type=jnp.float32)
    sigmoid_gate = jax.nn.sigmoid(gate_pre)
    activ = (gate_pre * sigmoid_gate * up_pre).astype(jnp.bfloat16)
    expert_out = jnp.dot(activ, w_down, preferred_element_type=jnp.float32).astype(jnp.bfloat16)
    grad_act = jnp.dot(grad_block, w_down.T, preferred_element_type=jnp.float32)
    grad_gate = (grad_act * up_pre * sigmoid_gate * (1.0 + gate_pre * (1.0 - sigmoid_gate))).astype(jnp.bfloat16)
    grad_up = (grad_act * gate_pre * sigmoid_gate).astype(jnp.bfloat16)
    expert_back = (jnp.dot(grad_gate, w_gate.T, preferred_element_type=jnp.float32)
                   + jnp.dot(grad_up, w_up.T, preferred_element_type=jnp.float32)).astype(jnp.bfloat16)
    return expert_out, expert_back


def reference(tokens, cotangent, expert_ids, probs, gate_weight, up_weight, down_weight):
    row_count = TOKENS * TOP_K
    most_rows = N_EXPERT * CAP
    flat_ids = expert_ids.reshape(row_count).astype(jnp.int32)
    sort_order = jnp.argsort(flat_ids, stable=True).astype(jnp.int32)
    counts = jnp.zeros((EXPERTS,), jnp.int32).at[flat_ids].add(1)
    starts = (jnp.cumsum(counts) - counts).astype(jnp.int32)
    padded = jnp.concatenate([sort_order, jnp.zeros((most_rows,), jnp.int32)])
    flat_probs = probs.reshape(row_count)

    def expert_step(state_pair, expert):
        summed, grad_sum = state_pair
        row_index = lax.dynamic_slice_in_dim(padded, starts[expert], most_rows)
        live_mask = jnp.arange(most_rows, dtype=jnp.int32) < counts[expert]
        token_index = (row_index // TOP_K).astype(jnp.int32)
        weight = jnp.where(live_mask, flat_probs[row_index], jnp.zeros_like(flat_probs[row_index]))
        expert_out, expert_back = expert_pass(tokens[token_index], cotangent[token_index],
                                              gate_weight[expert], up_weight[expert], down_weight[expert])
        summed = summed.at[token_index].add(weight[:, None] * expert_out.astype(jnp.float32))
        grad_sum = grad_sum.at[token_index].add(weight[:, None] * expert_back.astype(jnp.float32))
        return (summed, grad_sum), None

    start_pair = (jnp.zeros((TOKENS, D), jnp.float32), jnp.zeros((TOKENS, D), jnp.float32))
    (mixed, input_grad), _ = lax.scan(expert_step, start_pair, jnp.arange(EXPERTS, dtype=jnp.int32))
    return mixed, input_grad
```

```python
import functools

import jax
import jax.numpy as jnp
from jax import lax
from jax.experimental import pallas as pl
from jax.experimental.pallas import tpu as pltpu
from jax.sharding import PartitionSpec as P

MESH = pl.DeviceIdType.MESH
F32 = jnp.float32
BF16 = jnp.bfloat16
NT = (((1,), (1,)), ((), ()))

PY, PX, Z = 4, 4, 8
CAP = 6
CHUNK = 256


def moe_kernel(
    cfg, meta, tok, cot, wg_hbm, wu_hbm, wd_hbm, o_mix, o_grad,
    gat, stg, rcv, wg, wu, wd, pm, wt, wtmp, gu, ga, act, gg, pt, sb, mt,
    l_sem, w_sem, m_send, m_recv, zg_send, zg_recv, d_send, d_recv, d_self,
    r_send, r_recv, r_self, zr_send, zr_recv, credit,
):
    py, px, nz, cap, tk, top, dim, hid, el, cw = cfg
    nc = dim // cw
    nch = 2 * nc
    cols = py * px
    sl = nz * cap
    blk = el * sl
    nm = nz // 2
    np_ = nz - 1 - nm
    me = lax.axis_index("expert")
    z = lax.rem(me, nz)
    col = me // nz
    x = lax.rem(col, px)
    y = col // px

    def peer(c, zz):
        return {"expert": c * nz + zz}

    zup = lax.rem(z + 1, nz)
    zdn = lax.rem(z + nz - 1, nz)

    def colat(oy, ox):
        return lax.rem(y + oy, py) * px + lax.rem(x + ox, px)

    def own(ch, src, off):
        return pltpu.make_async_copy(
            src.at[:, pl.ds(pl.multiple_of(off * cw, cw), cw)], gat.at[ch, z], l_sem.at[ch]
        )

    for c in range(nc):
        own(c, tok, c).start()
    w_copies = [
        pltpu.make_async_copy(wg_hbm, wg, w_sem.at[0]),
        pltpu.make_async_copy(wu_hbm, wu, w_sem.at[1]),
        pltpu.make_async_copy(wd_hbm, wd, w_sem.at[2]),
    ]

    bar = pltpu.get_barrier_semaphore()

    def sig_plane(i, _):
        pl.semaphore_signal(
            bar, inc=1, device_id=peer(lax.rem(col + i, cols), z), device_id_type=MESH
        )
        return 0

    def sig_line(i, _):
        pl.semaphore_signal(
            bar, inc=1, device_id=peer(col, lax.rem(z + i, nz)), device_id_type=MESH
        )
        return 0

    lax.fori_loop(1, cols, sig_plane, 0)
    lax.fori_loop(1, nz, sig_line, 0)
    pl.semaphore_wait(bar, cols + nz - 2)

    def send_meta(i, _):
        pltpu.make_async_remote_copy(
            src_ref=meta, dst_ref=mt.at[z], send_sem=m_send.at[i - 1],
            recv_sem=m_recv.at[i - 1], device_id=peer(col, lax.rem(z + i, nz)),
            device_id_type=MESH,
        ).start()
        return 0

    lax.fori_loop(1, nz, send_meta, 0)

    def ring(ch, s):
        b = lax.rem(z - s + 1 + nz, nz)
        pltpu.make_async_remote_copy(
            src_ref=gat.at[ch, b], dst_ref=gat.at[ch, b], send_sem=zg_send.at[ch],
            recv_sem=zg_recv.at[ch, s - 1], device_id=peer(col, zup), device_id_type=MESH,
        ).start()
        if s <= np_:
            b = lax.rem(z + s - 1, nz)
            pltpu.make_async_remote_copy(
                src_ref=gat.at[ch, b], dst_ref=gat.at[ch, b], send_sem=zg_send.at[ch],
                recv_sem=zg_recv.at[ch, nm + s - 1], device_id=peer(col, zdn),
                device_id_type=MESH,
            ).start()

    def ring_wait(ch, s):
        b = lax.rem(z - s + nz, nz)
        pltpu.make_async_copy(gat.at[ch, b], gat.at[ch, b], zg_recv.at[ch, s - 1]).wait()
        if s <= np_:
            b = lax.rem(z + s, nz)
            pltpu.make_async_copy(
                gat.at[ch, b], gat.at[ch, b], zg_recv.at[ch, nm + s - 1]
            ).wait()

    def ring_first(ch):
        pltpu.make_async_copy(gat.at[ch, z], gat.at[ch, z], l_sem.at[ch]).wait()
        ring(ch, 1)

    def ring_event(ch, s):
        ring_wait(ch, s)
        if s < nm:
            ring(ch, s + 1)

    ring_first(0)
    ring_first(1)
    for c in range(nc):
        own(nc + c, cot, c).start()
    for w in w_copies:
        w.start()

    mt[z] = meta[...]

    def wait_meta(i, _):
        pltpu.make_async_copy(mt.at[z], mt.at[z], m_recv.at[i - 1]).wait()
        return 0

    lax.fori_loop(1, nz, wait_meta, 0)
    exs = cols * el
    before = (
        lax.broadcasted_iota(jnp.int32, (tk, tk), 0) < lax.broadcasted_iota(jnp.int32, (tk, tk), 1)
    ).astype(F32).astype(BF16)
    eye = (
        lax.broadcasted_iota(jnp.int32, (tk, tk), 0) == lax.broadcasted_iota(jnp.int32, (tk, tk), 1)
    ).astype(F32).astype(BF16)
    half = mt.shape[1] // 2

    def route(b, cnt):
        ids = mt[b, 0:half, :].astype(jnp.int32)
        pr = mt[b, half : 2 * half, :]
        lab = lax.broadcasted_iota(jnp.int32, (exs, tk), 0)
        member = jnp.zeros((exs, tk), F32)
        weight = jnp.zeros((exs, tk), F32)
        for k in range(top):
            idk = ids[k : k + 1, :]
            code = (idk // (el * nz)) * el + lax.rem(idk, el)
            code = jnp.where(lax.rem(idk // el, nz) == z, code, -1)
            hit = lab == code
            member = jnp.where(hit, 1.0, member)
            weight = jnp.where(hit, pr[k : k + 1, :], weight)
        rank = jnp.dot(member.astype(BF16), before, preferred_element_type=F32) + cnt
        rank = jnp.where(member > 0.5, rank, -1.0).astype(jnp.int32)
        hi = weight.astype(BF16).astype(F32)
        lo = weight - hi
        at = pl.ds(pl.multiple_of(b * tk, tk), tk)
        for ex in range(exs):
            j = lax.broadcasted_iota(jnp.int32, (sl, tk), 0)
            hit = j == rank[ex : ex + 1, :]
            rows = pl.ds(ex * sl, sl)
            pm[rows, at] = jnp.where(hit, 1.0, 0.0).astype(BF16)
            wtmp[0, rows, :] = jnp.where(hit, hi[ex : ex + 1, :], 0.0).astype(BF16)
            wtmp[1, rows, :] = jnp.where(hit, lo[ex : ex + 1, :], 0.0).astype(BF16)
        for i in range(2):
            wt[i, at, :] = lax.dot_general(
                eye, wtmp[i], NT, preferred_element_type=F32
            ).astype(BF16)
        return cnt + jnp.sum(member, axis=1, keepdims=True)

    lax.fori_loop(0, nz, route, jnp.zeros((exs, 1), F32))

    def ring_guarded(ch, s):
        @pl.when(ch < nch)
        def _():
            ring_event(ch, s)

    h1 = nm // 2
    for s in range(1, nm + 1):
        ring_event(0, s)
        if s <= h1:
            ring_event(1, s)
    ring_first(2)
    events = []
    for i in range(max(h1, nm - h1)):
        if h1 + 1 + i <= nm:
            events.append((1, h1 + 1 + i))
        if i < h1:
            events.append((2, 1 + i))
    for w in w_copies:
        w.wait()

    def acc_part(ch, q):
        ys = lax.rem(y - q + py, py)
        rows = pl.ds(ys * px, px)

        @pl.when(q == 0)
        def _():
            pltpu.make_async_copy(rcv.at[ch, col], rcv.at[ch, col], d_self.at[ch]).wait()
            pltpu.make_async_copy(
                rcv.at[ch, pl.ds(0, px - 1)], rcv.at[ch, pl.ds(0, px - 1)], d_recv.at[ch, q]
            ).wait()

        @pl.when(q > 0)
        def _():
            pltpu.make_async_copy(
                rcv.at[ch, pl.ds(0, px)], rcv.at[ch, pl.ds(0, px)], d_recv.at[ch, q]
            ).wait()

        def block(e):
            return rcv[ch, rows, pl.ds(e * sl, sl), :].reshape(px * sl, cw)

        @pl.when(ch < nc)
        def _():
            at = pl.ds(pl.multiple_of(ch * cw, cw), cw)
            for e in range(el):
                v = block(e)
                for h, w in ((0, wg), (1, wu)):
                    r = jnp.dot(v, w[e, at, :], preferred_element_type=F32)
                    gu[h, e, rows] += r.reshape(px, sl, hid)

        @pl.when(ch >= nc)
        def _():
            at = pl.ds(pl.multiple_of((ch - nc) * cw, cw), cw)
            for e in range(el):
                r = lax.dot_general(block(e), wd[e, :, at], NT, preferred_element_type=F32)
                ga[e, rows] += r.reshape(px, sl, hid)

    def wait_d_send(ch):
        pltpu.make_async_copy(
            stg.at[ch, pl.ds(0, cols - 1)], stg.at[ch, pl.ds(0, cols - 1)], d_send.at[ch]
        ).wait()

    gu[...] = jnp.zeros_like(gu)
    ga[...] = jnp.zeros_like(ga)

    def dispatch(i, _):
        ch = i // py
        q = lax.rem(i, py)
        for k, (d, s) in enumerate(events):
            @pl.when(q == k * py // len(events))
            def _():
                ring_guarded(ch + d, s)

        @pl.when((q == py - 1) & (ch + 3 < nch))
        def _():
            ring_first(ch + 3)

        @pl.when((q == 0) & (ch >= 2))
        def _():
            wait_d_send(ch - 2)

        yd = lax.rem(y + q, py)
        rows = pl.ds(pl.multiple_of(yd * (px * blk), px * blk), px * blk)
        packed = jnp.dot(
            pm[rows, :], gat[ch].reshape(nz * tk, cw), preferred_element_type=F32
        )
        stg[ch, pl.ds(yd * px, px)] = packed.astype(BF16).reshape(px, blk, cw)

        @pl.when(ch >= 2)
        def _():
            acc_part(ch - 2, q)

        for ox in range(px):
            d = colat(q, ox)

            def remote():
                pltpu.make_async_remote_copy(
                    src_ref=stg.at[ch, d], dst_ref=rcv.at[ch, col], send_sem=d_send.at[ch],
                    recv_sem=d_recv.at[ch, q], device_id=peer(d, z), device_id_type=MESH,
                ).start()

            if ox == 0:
                @pl.when(q == 0)
                def _():
                    pltpu.make_async_copy(
                        stg.at[ch, col], rcv.at[ch, col], d_self.at[ch]
                    ).start()

                @pl.when(q > 0)
                def _():
                    remote()
            else:
                remote()
        return 0

    lax.fori_loop(0, nch * py, dispatch, 0)

    def wait_zg(ch, _):
        pltpu.make_async_copy(
            gat.at[ch, pl.ds(0, nz - 1)], gat.at[ch, pl.ds(0, nz - 1)], zg_send.at[ch]
        ).wait()
        return 0

    lax.fori_loop(0, nch, wait_zg, 0)
    for zz in (zup, zdn):
        pl.semaphore_signal(credit, inc=1, device_id=peer(col, zz), device_id_type=MESH)

    def forward_act(p, _):
        for e in range(el):
            g = gu[0, e, p]
            act[e, p] = (g * jax.nn.sigmoid(g) * gu[1, e, p]).astype(BF16)
        return 0

    lax.fori_loop(0, cols, forward_act, 0)

    def backward_act(p, _):
        for e in range(el):
            g = gu[0, e, p]
            sig = jax.nn.sigmoid(g)
            d = ga[e, p]
            gg[0, e, p] = (d * gu[1, e, p] * sig * (1.0 + g * (1.0 - sig))).astype(BF16)
            gg[1, e, p] = (d * g * sig).astype(BF16)
        return 0

    def expert_part(r, q):
        rows = pl.ds(lax.rem(y + q, py) * px, px)

        @pl.when(r < nc)
        def _():
            at = pl.ds(pl.multiple_of(r * cw, cw), cw)
            for e in range(el):
                v = act[e, rows].reshape(px * sl, hid)
                o = jnp.dot(v, wd[e, :, at], preferred_element_type=F32)
                rcv[r, rows, pl.ds(e * sl, sl), :] = o.astype(BF16).reshape(px, sl, cw)

        @pl.when(r >= nc)
        def _():
            at = pl.ds(pl.multiple_of((r - nc) * cw, cw), cw)
            for e in range(el):
                o = lax.dot_general(
                    gg[0, e, rows].reshape(px * sl, hid), wg[e, at, :], NT,
                    preferred_element_type=F32,
                ) + lax.dot_general(
                    gg[1, e, rows].reshape(px * sl, hid), wu[e, at, :], NT,
                    preferred_element_type=F32,
                )
                rcv[r, rows, pl.ds(e * sl, sl), :] = o.astype(BF16).reshape(px, sl, cw)

    bq = nz // py

    def combine_part(c, q):
        @pl.when(q == 0)
        def _():
            pltpu.make_async_copy(stg.at[c, col], stg.at[c, col], r_self.at[c]).wait()
            for k in range(py):
                n = px - 1 if k == 0 else px
                pltpu.make_async_copy(
                    stg.at[c, pl.ds(0, n)], stg.at[c, pl.ds(0, n)], r_recv.at[c, k]
                ).wait()

        rows = pl.ds(pl.multiple_of(q * (bq * tk), bq * tk), bq * tk)
        v = stg[c].reshape(cols * blk, cw)
        o = jnp.dot(wt[0, rows, :], v, preferred_element_type=F32) + jnp.dot(
            wt[1, rows, :], v, preferred_element_type=F32
        )
        pt[lax.rem(c, 3), pl.ds(q * bq, bq)] = o.reshape(bq, tk, cw)

    def sum_send(c, s, dn):
        slot = lax.rem(c, 3)
        i = s - 1 if dn else nm + s - 1
        b = lax.rem(z - nm + s - 1 + nz, nz) if dn else lax.rem(z + np_ + 1 - s, nz)
        v = pt[slot, b]
        if s > 1:
            v = v + gat[c, i - 1].astype(F32)
        sb[slot, i] = v.astype(BF16)
        pltpu.make_async_remote_copy(
            src_ref=sb.at[slot, i], dst_ref=gat.at[c, i], send_sem=zr_send.at[c],
            recv_sem=zr_recv.at[c, i], device_id=peer(col, zdn if dn else zup),
            device_id_type=MESH,
        ).start()

    def sum_wait(c, i):
        pltpu.make_async_copy(gat.at[c, i], gat.at[c, i], zr_recv.at[c, i]).wait()

    def sum_event(c, s):
        if s > 1:
            sum_wait(c, s - 2)
            if s - 1 <= np_:
                sum_wait(c, nm + s - 2)
        if s <= nm:
            sum_send(c, s, True)
        if s <= np_:
            sum_send(c, s, False)
        if s == nm + 1:
            slot = lax.rem(c, 3)
            total = pt[slot, z] + gat[c, nm - 1].astype(F32)
            if np_ > 0:
                total = total + gat[c, nm + np_ - 1].astype(F32)

            @pl.when(c < nc)
            def _():
                o_mix[:, pl.ds(pl.multiple_of(c * cw, cw), cw)] = total

            @pl.when(c >= nc)
            def _():
                o_grad[:, pl.ds(pl.multiple_of((c - nc) * cw, cw), cw)] = total

            pltpu.make_async_copy(
                gat.at[c, pl.ds(0, nz - 1)], gat.at[c, pl.ds(0, nz - 1)], zr_send.at[c]
            ).wait()

    sums = []
    for s in range(1, nm + 2):
        tick = (s - 1) * max(1, 2 * py // nm // 1) if nm < 4 else (s - 1) * 2
        tick = min(tick, 2 * py)
        sums.append((3 + tick // py, tick % py, s))
    last = nch + max(d for d, _, _ in sums)

    def give_back(i, _):
        r = i // py
        q = lax.rem(i, py)

        @pl.when((r == 3) & (q == 0))
        def _():
            pl.semaphore_wait(credit, 2)

        for d, k, s in sorted(sums, key=lambda v: (-v[0], v[1])):
            @pl.when((q == k) & (r >= d) & (r - d < nch))
            def _():
                sum_event(r - d, s)

        @pl.when((q == 0) & (r < 2))
        def _():
            wait_d_send(nch - 2 + r)

        @pl.when(r < nch)
        def _():
            expert_part(r, q)

        @pl.when(r < 2)
        def _():
            acc_part(nch - 2 + r, q)

            @pl.when((r == 1) & (q == py - 1))
            def _():
                lax.fori_loop(0, cols, backward_act, 0)

        @pl.when((r >= 2) & (r - 2 < nch))
        def _():
            combine_part(r - 2, q)

        @pl.when(r < nch)
        def _():
            for ox in range(px):
                d = colat(q, ox)

                def remote():
                    pltpu.make_async_remote_copy(
                        src_ref=rcv.at[r, d], dst_ref=stg.at[r, col], send_sem=r_send.at[r],
                        recv_sem=r_recv.at[r, q], device_id=peer(d, z), device_id_type=MESH,
                    ).start()

                if ox == 0:
                    @pl.when(q == 0)
                    def _():
                        pltpu.make_async_copy(
                            rcv.at[r, col], stg.at[r, col], r_self.at[r]
                        ).start()

                    @pl.when(q > 0)
                    def _():
                        remote()
                else:
                    remote()

        return 0

    lax.fori_loop(0, last * py, give_back, 0)

    def finish(ch, _):
        pltpu.make_async_copy(
            rcv.at[ch, pl.ds(0, cols - 1)], rcv.at[ch, pl.ds(0, cols - 1)], r_send.at[ch]
        ).wait()
        return 0

    lax.fori_loop(0, nch, finish, 0)

    def finish_meta(i, _):
        pltpu.make_async_copy(mt.at[z], mt.at[z], m_send.at[i - 1]).wait()
        return 0

    lax.fori_loop(1, nz, finish_meta, 0)


def on_device(cfg, tokens, cotangent, expert_ids, probs, gate_weight, up_weight, down_weight):
    py, px, nz, cap, tk, top, dim, hid, el, cw = cfg
    nch = 2 * (dim // cw)
    cols = py * px
    sl = nz * cap
    blk = el * sl
    half = -(-top // 8) * 8
    pad = ((0, half - top), (0, 0))
    meta = jnp.concatenate(
        [jnp.pad(expert_ids.T.astype(F32), pad), jnp.pad(probs.T, pad)], axis=0
    )
    vm = pl.BlockSpec(memory_space=pltpu.VMEM)
    hbm = pl.BlockSpec(memory_space=pl.ANY)
    dma = pltpu.SemaphoreType.DMA
    return pl.pallas_call(
        functools.partial(moe_kernel, cfg),
        out_shape=(
            jax.ShapeDtypeStruct((tk, dim), F32),
            jax.ShapeDtypeStruct((tk, dim), F32),
        ),
        in_specs=[vm, hbm, hbm, hbm, hbm, hbm],
        out_specs=(vm, vm),
        scratch_shapes=[
            pltpu.VMEM((nch, nz, tk, cw), BF16),
            pltpu.VMEM((nch, cols, blk, cw), BF16),
            pltpu.VMEM((nch, cols, blk, cw), BF16),
            pltpu.VMEM(gate_weight.shape, BF16),
            pltpu.VMEM(up_weight.shape, BF16),
            pltpu.VMEM(down_weight.shape, BF16),
            pltpu.VMEM((cols * blk, nz * tk), BF16),
            pltpu.VMEM((2, nz * tk, cols * blk), BF16),
            pltpu.VMEM((2, cols * blk, tk), BF16),
            pltpu.VMEM((2, el, cols, sl, hid), F32),
            pltpu.VMEM((el, cols, sl, hid), F32),
            pltpu.VMEM((el, cols, sl, hid), BF16),
            pltpu.VMEM((2, el, cols, sl, hid), BF16),
            pltpu.VMEM((3, nz, tk, cw), F32),
            pltpu.VMEM((3, nz - 1, tk, cw), BF16),
            pltpu.VMEM((nz, 2 * half, tk), F32),
            dma((nch,)),
            dma((3,)),
            dma((nz - 1,)),
            dma((nz - 1,)),
            dma((nch,)),
            dma((nch, nz - 1)),
            dma((nch,)),
            dma((nch, py)),
            dma((nch,)),
            dma((nch,)),
            dma((nch, py)),
            dma((nch,)),
            dma((nch,)),
            dma((nch, nz - 1)),
            pltpu.SemaphoreType.REGULAR,
        ],
        compiler_params=pltpu.CompilerParams(
            collective_id=0, has_side_effects=True, vmem_limit_bytes=67043328
        ),
        name="moe",
    )(meta, tokens, cotangent, gate_weight, up_weight, down_weight)


def solution(mesh):
    rows = P(("dp", "expert"), None)
    cubes = P(("dp", "expert"), None, None)

    def body(tokens, cotangent, expert_ids, probs, gate_weight, up_weight, down_weight):
        tk, dim = tokens.shape
        cfg = (PY, PX, Z, CAP, tk, expert_ids.shape[1], dim, gate_weight.shape[2],
               gate_weight.shape[0], min(CHUNK, dim // 2))
        return on_device(
            cfg, tokens, cotangent, expert_ids, probs, gate_weight, up_weight, down_weight
        )

    return jax.shard_map(
        body, mesh=mesh, in_specs=(rows,) * 4 + (cubes,) * 3, out_specs=(rows, rows),
        check_vma=False,
    )
```

```python
import functools

import jax
import jax.numpy as jnp
from jax import lax
from jax.experimental import pallas as pl
from jax.experimental.pallas import tpu as pltpu
from jax.sharding import PartitionSpec as P

MESH = pl.DeviceIdType.MESH
F32 = jnp.float32
BF16 = jnp.bfloat16
NT = (((1,), (1,)), ((), ()))

PY, PX, Z = 4, 4, 8
CAP = 6
CHUNK = 256
STRIDE = 3


def moe_kernel(
    cfg, meta, tok, cot, wg_hbm, wu_hbm, wd_hbm, o_mix, o_grad,
    gat, stg, rcv, wg, wu, wd, pm, wt, gu, ga, act, gg, pt, sb, ost, mt,
    l_sem, w_sem, m_send, m_recv, zg_send, zg_recv, d_send, d_recv, d_self,
    r_send, r_recv, r_self, zr_send, zr_recv, o_sem, credit,
):
    py, px, nz, cap, tk, top, dim, hid, el, cw = cfg
    nc = dim // cw
    nch = 2 * nc
    cols = py * px
    sl = nz * cap
    blk = el * sl
    nm = nz // 2
    np_ = nz - 1 - nm
    slots = pt.shape[0]
    me = lax.axis_index("expert")
    z = lax.rem(me, nz)
    col = me // nz
    x = lax.rem(col, px)
    y = col // px

    def peer(c, zz):
        return {"expert": c * nz + zz}

    sense = 1 - 2 * lax.rem(lax.axis_index("dp"), 2)

    def along(n):
        return lax.rem(z + sense * n + 2 * nz, nz)

    zup = along(1)
    zdn = along(-1)

    def colat(oy, ox):
        return lax.rem(y + oy, py) * px + lax.rem(x + ox, px)

    def own(ch, src, off):
        return pltpu.make_async_copy(
            src.at[:, pl.ds(pl.multiple_of(off * cw, cw), cw)], gat.at[ch, z], l_sem.at[ch]
        )

    for c in range(nc):
        own(c, tok, c).start()
    w_copies = [
        pltpu.make_async_copy(wg_hbm, wg, w_sem.at[0]),
        pltpu.make_async_copy(wu_hbm, wu, w_sem.at[1]),
        pltpu.make_async_copy(wd_hbm, wd, w_sem.at[2]),
    ]

    bar = pltpu.get_barrier_semaphore()

    def sig_plane(i, _):
        pl.semaphore_signal(
            bar, inc=1, device_id=peer(lax.rem(col + i, cols), z), device_id_type=MESH
        )
        return 0

    def sig_line(i, _):
        pl.semaphore_signal(
            bar, inc=1, device_id=peer(col, lax.rem(z + i, nz)), device_id_type=MESH
        )
        return 0

    lax.fori_loop(1, cols, sig_plane, 0)
    lax.fori_loop(1, nz, sig_line, 0)
    pl.semaphore_wait(bar, cols + nz - 2)

    def send_meta(i, _):
        pltpu.make_async_remote_copy(
            src_ref=meta, dst_ref=mt.at[z], send_sem=m_send.at[i - 1],
            recv_sem=m_recv.at[i - 1], device_id=peer(col, lax.rem(z + i, nz)),
            device_id_type=MESH,
        ).start()
        return 0

    lax.fori_loop(1, nz, send_meta, 0)

    def ring(ch, s):
        b = along(1 - s)
        pltpu.make_async_remote_copy(
            src_ref=gat.at[ch, b], dst_ref=gat.at[ch, b], send_sem=zg_send.at[ch],
            recv_sem=zg_recv.at[ch, s - 1], device_id=peer(col, zup), device_id_type=MESH,
        ).start()
        if s <= np_:
            b = along(s - 1)
            pltpu.make_async_remote_copy(
                src_ref=gat.at[ch, b], dst_ref=gat.at[ch, b], send_sem=zg_send.at[ch],
                recv_sem=zg_recv.at[ch, nm + s - 1], device_id=peer(col, zdn),
                device_id_type=MESH,
            ).start()

    def ring_wait(ch, s):
        b = along(-s)
        pltpu.make_async_copy(gat.at[ch, b], gat.at[ch, b], zg_recv.at[ch, s - 1]).wait()
        if s <= np_:
            b = along(s)
            pltpu.make_async_copy(
                gat.at[ch, b], gat.at[ch, b], zg_recv.at[ch, nm + s - 1]
            ).wait()

    def ring_first(ch):
        pltpu.make_async_copy(gat.at[ch, z], gat.at[ch, z], l_sem.at[ch]).wait()
        ring(ch, 1)

    def ring_event(ch, s):
        ring_wait(ch, s)
        if s < nm:
            ring(ch, s + 1)

    steps = [(-1 - STRIDE * (nm - s), s) for s in range(nm + 1)]
    early = sorted(
        (t + py * ch, ch, s) for t, s in steps for ch in range(nch) if t + py * ch < 0
    )
    steps = sorted((t % py, -(t // py), s) for t, s in steps)

    def step(ch, s):
        if s == 0:
            ring_first(ch)
        else:
            ring_event(ch, s)

    step(*early[0][1:])
    early = early[1:]
    for c in range(nc):
        own(nc + c, cot, c).start()
    for w in w_copies:
        w.start()

    mt[z] = meta[...]

    def wait_meta(i, _):
        pltpu.make_async_copy(mt.at[z], mt.at[z], m_recv.at[i - 1]).wait()
        return 0

    lax.fori_loop(1, nz, wait_meta, 0)
    exs = cols * el
    before = (
        lax.broadcasted_iota(jnp.int32, (tk, tk), 0) < lax.broadcasted_iota(jnp.int32, (tk, tk), 1)
    ).astype(F32).astype(BF16)
    eye = (
        lax.broadcasted_iota(jnp.int32, (tk, tk), 0) == lax.broadcasted_iota(jnp.int32, (tk, tk), 1)
    ).astype(F32).astype(BF16)
    half = mt.shape[1] // 2

    def route(b, cnt):
        ids = mt[b, 0:half, :].astype(jnp.int32)
        pr = mt[b, half : 2 * half, :]
        lab = lax.broadcasted_iota(jnp.int32, (exs, tk), 0)
        member = jnp.zeros((exs, tk), F32)
        weight = jnp.zeros((exs, tk), F32)
        for k in range(top):
            idk = ids[k : k + 1, :]
            code = (idk // (el * nz)) * el + lax.rem(idk, el)
            code = jnp.where(lax.rem(idk // el, nz) == z, code, -1)
            hit = lab == code
            member = jnp.where(hit, 1.0, member)
            weight = jnp.where(hit, pr[k : k + 1, :], weight)
        rank = jnp.dot(member.astype(BF16), before, preferred_element_type=F32) + cnt
        rank = jnp.where(member > 0.5, rank, -1.0).astype(jnp.int32)
        hi = weight.astype(BF16).astype(F32)
        lo = weight - hi
        at = pl.ds(pl.multiple_of(b * tk, tk), tk)
        for ex in range(exs):
            j = lax.broadcasted_iota(jnp.int32, (sl, tk), 0)
            hit = j == rank[ex : ex + 1, :]
            rows = pl.ds(ex * sl, sl)
            pm[rows, at] = jnp.where(hit, 1.0, 0.0).astype(BF16)
            for i, w in enumerate((hi, lo)):
                stg[nch - 1, ex // el, pl.ds((ex % el) * sl, sl), pl.ds(i * tk, tk)] = (
                    jnp.where(hit, w[ex : ex + 1, :], 0.0).astype(BF16)
                )
        for i in range(2):
            wt[i, at, :] = lax.dot_general(
                eye, stg[nch - 1, :, :, pl.ds(i * tk, tk)].reshape(cols * blk, tk), NT,
                preferred_element_type=F32,
            ).astype(BF16)
        return cnt + jnp.sum(member, axis=1, keepdims=True)

    def route_step(b, cnt):
        for n, (_, ch, s) in enumerate(early):
            @pl.when(b == (n * nz) // len(early))
            def _():
                step(ch, s)
        return route(b, cnt)

    lax.fori_loop(0, nz, route_step, jnp.zeros((exs, 1), F32))
    for w in w_copies:
        w.wait()

    def acc_part(ch, q):
        ys = lax.rem(y - q + py, py)
        rows = pl.ds(ys * px, px)

        @pl.when(q == 0)
        def _():
            pltpu.make_async_copy(rcv.at[ch, col], rcv.at[ch, col], d_self.at[ch]).wait()
            pltpu.make_async_copy(
                rcv.at[ch, pl.ds(0, px - 1)], rcv.at[ch, pl.ds(0, px - 1)], d_recv.at[ch, q]
            ).wait()

        @pl.when(q > 0)
        def _():
            pltpu.make_async_copy(
                rcv.at[ch, pl.ds(0, px)], rcv.at[ch, pl.ds(0, px)], d_recv.at[ch, q]
            ).wait()

        def block(e):
            return rcv[ch, rows, pl.ds(e * sl, sl), :].reshape(px * sl, cw)

        @pl.when(ch < nc)
        def _():
            at = pl.ds(pl.multiple_of(ch * cw, cw), cw)
            for e in range(el):
                v = block(e)
                for h, w in ((0, wg), (1, wu)):
                    r = jnp.dot(v, w[e, at, :], preferred_element_type=F32)
                    gu[h, e, rows] += r.reshape(px, sl, hid)

        @pl.when(ch >= nc)
        def _():
            at = pl.ds(pl.multiple_of((ch - nc) * cw, cw), cw)
            for e in range(el):
                r = lax.dot_general(block(e), wd[e, :, at], NT, preferred_element_type=F32)
                ga[e, rows] += r.reshape(px, sl, hid)

    def wait_d_send(ch):
        pltpu.make_async_copy(
            stg.at[ch, pl.ds(0, cols - 1)], stg.at[ch, pl.ds(0, cols - 1)], d_send.at[ch]
        ).wait()

    gu[...] = jnp.zeros_like(gu)
    ga[...] = jnp.zeros_like(ga)

    def dispatch(i, _):
        ch = i // py
        q = lax.rem(i, py)
        for k, d, s in steps:
            @pl.when((q == k) & (ch + d < nch))
            def _():
                step(ch + d, s)

        @pl.when((q == 0) & (ch >= 2))
        def _():
            wait_d_send(ch - 2)

        yd = lax.rem(y + q, py)
        rows = pl.ds(pl.multiple_of(yd * (px * blk), px * blk), px * blk)
        packed = jnp.dot(
            pm[rows, :], gat[ch].reshape(nz * tk, cw), preferred_element_type=F32
        )
        stg[ch, pl.ds(yd * px, px)] = packed.astype(BF16).reshape(px, blk, cw)

        @pl.when(ch >= 2)
        def _():
            acc_part(ch - 2, q)

        for ox in range(px):
            d = colat(q, ox)

            def remote():
                pltpu.make_async_remote_copy(
                    src_ref=stg.at[ch, d], dst_ref=rcv.at[ch, col], send_sem=d_send.at[ch],
                    recv_sem=d_recv.at[ch, q], device_id=peer(d, z), device_id_type=MESH,
                ).start()

            if ox == 0:
                @pl.when(q == 0)
                def _():
                    pltpu.make_async_copy(
                        stg.at[ch, col], rcv.at[ch, col], d_self.at[ch]
                    ).start()

                @pl.when(q > 0)
                def _():
                    remote()
            else:
                remote()
        return 0

    lax.fori_loop(0, nch * py, dispatch, 0)

    def wait_zg(ch, _):
        pltpu.make_async_copy(
            gat.at[ch, pl.ds(0, nz - 1)], gat.at[ch, pl.ds(0, nz - 1)], zg_send.at[ch]
        ).wait()
        return 0

    lax.fori_loop(0, nch, wait_zg, 0)
    for zz in (zup, zdn):
        pl.semaphore_signal(credit, inc=1, device_id=peer(col, zz), device_id_type=MESH)

    def forward_act(p, _):
        for e in range(el):
            g = gu[0, e, p]
            act[e, p] = (g * jax.nn.sigmoid(g) * gu[1, e, p]).astype(BF16)
        return 0

    lax.fori_loop(0, cols, forward_act, 0)

    def backward_act(p, _):
        for e in range(el):
            g = gu[0, e, p]
            sig = jax.nn.sigmoid(g)
            d = ga[e, p]
            gg[0, e, p] = (d * gu[1, e, p] * sig * (1.0 + g * (1.0 - sig))).astype(BF16)
            gg[1, e, p] = (d * g * sig).astype(BF16)
        return 0

    def expert_part(r, q):
        rows = pl.ds(lax.rem(y + q, py) * px, px)

        @pl.when(r < nc)
        def _():
            at = pl.ds(pl.multiple_of(r * cw, cw), cw)
            for e in range(el):
                v = act[e, rows].reshape(px * sl, hid)
                o = jnp.dot(v, wd[e, :, at], preferred_element_type=F32)
                rcv[r, rows, pl.ds(e * sl, sl), :] = o.astype(BF16).reshape(px, sl, cw)

        @pl.when(r >= nc)
        def _():
            at = pl.ds(pl.multiple_of((r - nc) * cw, cw), cw)
            for e in range(el):
                o = lax.dot_general(
                    gg[0, e, rows].reshape(px * sl, hid), wg[e, at, :], NT,
                    preferred_element_type=F32,
                ) + lax.dot_general(
                    gg[1, e, rows].reshape(px * sl, hid), wu[e, at, :], NT,
                    preferred_element_type=F32,
                )
                rcv[r, rows, pl.ds(e * sl, sl), :] = o.astype(BF16).reshape(px, sl, cw)

    bq = nz // py

    def combine_part(c, q):
        @pl.when(q == 0)
        def _():
            pltpu.make_async_copy(stg.at[c, col], stg.at[c, col], r_self.at[c]).wait()
            for k in range(py):
                n = px - 1 if k == 0 else px
                pltpu.make_async_copy(
                    stg.at[c, pl.ds(0, n)], stg.at[c, pl.ds(0, n)], r_recv.at[c, k]
                ).wait()

        rows = pl.ds(pl.multiple_of(q * (bq * tk), bq * tk), bq * tk)
        v = stg[c].reshape(cols * blk, cw)
        o = jnp.dot(wt[0, rows, :], v, preferred_element_type=F32) + jnp.dot(
            wt[1, rows, :], v, preferred_element_type=F32
        )
        pt[lax.rem(c, slots), pl.ds(q * bq, bq)] = o.reshape(bq, tk, cw)

    def sum_send(c, s, dn):
        slot = lax.rem(c, slots)
        i = s - 1 if dn else nm + s - 1
        b = along(s - 1 - nm) if dn else along(np_ + 1 - s)
        v = pt[slot, b]
        if s > 1:
            v = v + gat[c, i - 1].astype(F32)
        sb[slot, i] = v.astype(BF16)
        pltpu.make_async_remote_copy(
            src_ref=sb.at[slot, i], dst_ref=gat.at[c, i], send_sem=zr_send.at[c],
            recv_sem=zr_recv.at[c, i], device_id=peer(col, zdn if dn else zup),
            device_id_type=MESH,
        ).start()

    def sum_wait(c, i):
        pltpu.make_async_copy(gat.at[c, i], gat.at[c, i], zr_recv.at[c, i]).wait()

    def out_copy(dst, c, o):
        at = pl.ds(pl.multiple_of(c * cw, cw), cw)
        return pltpu.make_async_copy(ost.at[o], dst.at[:, at], o_sem.at[o])

    def sum_event(c, s):
        if s > 1:
            sum_wait(c, s - 2)
            if s - 1 <= np_:
                sum_wait(c, nm + s - 2)
        if s <= nm:
            sum_send(c, s, True)
        if s <= np_:
            sum_send(c, s, False)
        if s == nm + 1:
            slot = lax.rem(c, slots)
            total = pt[slot, z] + gat[c, nm - 1].astype(F32)
            if np_ > 0:
                total = total + gat[c, nm + np_ - 1].astype(F32)

            o = lax.rem(c, 2)

            @pl.when(c >= 2)
            def _():
                out_copy(o_mix, 0, o).wait()

            ost[o] = total

            @pl.when(c < nc)
            def _():
                out_copy(o_mix, c, o).start()

            @pl.when(c >= nc)
            def _():
                out_copy(o_grad, c - nc, o).start()

            pltpu.make_async_copy(
                gat.at[c, pl.ds(0, nz - 1)], gat.at[c, pl.ds(0, nz - 1)], zr_send.at[c]
            ).wait()

    sums = []
    for s in range(1, nm + 2):
        tick = STRIDE * (s - 1)
        sums.append((3 + tick // py, tick % py, s))
    last = nch + max(d for d, _, _ in sums)

    def give_back(i, _):
        r = i // py
        q = lax.rem(i, py)

        @pl.when((r == 3) & (q == 0))
        def _():
            pl.semaphore_wait(credit, 2)

        for d, k, s in sorted(sums, key=lambda v: (-v[0], v[1])):
            @pl.when((q == k) & (r >= d) & (r - d < nch))
            def _():
                sum_event(r - d, s)

        @pl.when((q == 0) & (r < 2))
        def _():
            wait_d_send(nch - 2 + r)

        @pl.when(r < nch)
        def _():
            expert_part(r, q)

        @pl.when(r < 2)
        def _():
            acc_part(nch - 2 + r, q)

            @pl.when((r == 1) & (q == py - 1))
            def _():
                lax.fori_loop(0, cols, backward_act, 0)

        @pl.when((r >= 2) & (r - 2 < nch))
        def _():
            combine_part(r - 2, q)

        @pl.when(r < nch)
        def _():
            for ox in range(px):
                d = colat(q, ox)

                def remote():
                    pltpu.make_async_remote_copy(
                        src_ref=rcv.at[r, d], dst_ref=stg.at[r, col], send_sem=r_send.at[r],
                        recv_sem=r_recv.at[r, q], device_id=peer(d, z), device_id_type=MESH,
                    ).start()

                if ox == 0:
                    @pl.when(q == 0)
                    def _():
                        pltpu.make_async_copy(
                            rcv.at[r, col], stg.at[r, col], r_self.at[r]
                        ).start()

                    @pl.when(q > 0)
                    def _():
                        remote()
                else:
                    remote()

        return 0

    lax.fori_loop(0, last * py, give_back, 0)

    def finish(ch, _):
        pltpu.make_async_copy(
            rcv.at[ch, pl.ds(0, cols - 1)], rcv.at[ch, pl.ds(0, cols - 1)], r_send.at[ch]
        ).wait()
        return 0

    lax.fori_loop(0, nch, finish, 0)

    for o in range(2):
        out_copy(o_grad, 0, o).wait()

    def finish_meta(i, _):
        pltpu.make_async_copy(mt.at[z], mt.at[z], m_send.at[i - 1]).wait()
        return 0

    lax.fori_loop(1, nz, finish_meta, 0)


def on_device(cfg, tokens, cotangent, expert_ids, probs, gate_weight, up_weight, down_weight):
    py, px, nz, cap, tk, top, dim, hid, el, cw = cfg
    nch = 2 * (dim // cw)
    cols = py * px
    sl = nz * cap
    blk = el * sl
    slots = 1 + -(-(STRIDE * (nz // 2)) // py)
    half = -(-top // 8) * 8
    pad = ((0, half - top), (0, 0))
    meta = jnp.concatenate(
        [jnp.pad(expert_ids.T.astype(F32), pad), jnp.pad(probs.T, pad)], axis=0
    )
    vm = pl.BlockSpec(memory_space=pltpu.VMEM)
    hbm = pl.BlockSpec(memory_space=pl.ANY)
    dma = pltpu.SemaphoreType.DMA
    return pl.pallas_call(
        functools.partial(moe_kernel, cfg),
        out_shape=(
            jax.ShapeDtypeStruct((tk, dim), F32),
            jax.ShapeDtypeStruct((tk, dim), F32),
        ),
        in_specs=[vm, hbm, hbm, hbm, hbm, hbm],
        out_specs=(hbm, hbm),
        scratch_shapes=[
            pltpu.VMEM((nch, nz, tk, cw), BF16),
            pltpu.VMEM((nch, cols, blk, cw), BF16),
            pltpu.VMEM((nch, cols, blk, cw), BF16),
            pltpu.VMEM(gate_weight.shape, BF16),
            pltpu.VMEM(up_weight.shape, BF16),
            pltpu.VMEM(down_weight.shape, BF16),
            pltpu.VMEM((cols * blk, nz * tk), BF16),
            pltpu.VMEM((2, nz * tk, cols * blk), BF16),
            pltpu.VMEM((2, el, cols, sl, hid), F32),
            pltpu.VMEM((el, cols, sl, hid), F32),
            pltpu.VMEM((el, cols, sl, hid), BF16),
            pltpu.VMEM((2, el, cols, sl, hid), BF16),
            pltpu.VMEM((slots, nz, tk, cw), F32),
            pltpu.VMEM((slots, nz - 1, tk, cw), BF16),
            pltpu.VMEM((2, tk, cw), F32),
            pltpu.VMEM((nz, 2 * half, tk), F32),
            dma((nch,)),
            dma((3,)),
            dma((nz - 1,)),
            dma((nz - 1,)),
            dma((nch,)),
            dma((nch, nz - 1)),
            dma((nch,)),
            dma((nch, py)),
            dma((nch,)),
            dma((nch,)),
            dma((nch, py)),
            dma((nch,)),
            dma((nch,)),
            dma((nch, nz - 1)),
            dma((2,)),
            pltpu.SemaphoreType.REGULAR,
        ],
        compiler_params=pltpu.CompilerParams(
            collective_id=0, has_side_effects=True, vmem_limit_bytes=67043328
        ),
        name="moe",
    )(meta, tokens, cotangent, gate_weight, up_weight, down_weight)


def solution(mesh):
    rows = P(("dp", "expert"), None)
    cubes = P(("dp", "expert"), None, None)

    def body(tokens, cotangent, expert_ids, probs, gate_weight, up_weight, down_weight):
        tk, dim = tokens.shape
        cfg = (PY, PX, Z, CAP, tk, expert_ids.shape[1], dim, gate_weight.shape[2],
               gate_weight.shape[0], min(CHUNK, dim // 2))
        return on_device(
            cfg, tokens, cotangent, expert_ids, probs, gate_weight, up_weight, down_weight
        )

    return jax.shard_map(
        body, mesh=mesh, in_specs=(rows,) * 4 + (cubes,) * 3, out_specs=(rows, rows),
        check_vma=False,
    )
```

```python
import functools

import jax
import jax.numpy as jnp
from jax import lax
from jax.experimental import pallas as pl
from jax.experimental.pallas import tpu as pltpu
from jax.sharding import PartitionSpec as P

MESH = pl.DeviceIdType.MESH
F32 = jnp.float32
BF16 = jnp.bfloat16
NT = (((1,), (1,)), ((), ()))

PY, PX, Z = 4, 4, 8
CAP = 6
CHUNK = 256
STRIDE = 3
STRIDE_SUM = 3
LAG = 4


def moe_kernel(
    cfg, meta, tok, cot, wg_hbm, wu_hbm, wd_hbm, o_mix, o_grad,
    gat, stg, rcv, wg, wu, wd, pm, wt, gu, ga, act, gg, pt, sb, ost, mt,
    l_sem, w_sem, m_send, m_recv, zg_send, zg_recv, d_send, d_recv, d_self,
    r_send, r_recv, r_self, zr_send, zr_recv, o_sem, credit,
):
    py, px, nz, cap, tk, top, dim, hid, el, cw = cfg
    nc = dim // cw
    nch = 2 * nc
    cols = py * px
    sl = nz * cap
    blk = el * sl
    nm = nz // 2
    np_ = nz - 1 - nm
    slots = pt.shape[0]
    me = lax.axis_index("expert")
    z = lax.rem(me, nz)
    col = me // nz
    x = lax.rem(col, px)
    y = col // px

    def peer(c, zz):
        return {"expert": c * nz + zz}

    sense = 1 - 2 * lax.rem(lax.axis_index("dp"), 2)

    def along(n):
        return lax.rem(z + sense * n + 2 * nz, nz)

    zup = along(1)
    zdn = along(-1)

    def colat(oy, ox):
        return lax.rem(y + oy, py) * px + lax.rem(x + ox, px)

    def own(ch, src, off):
        return pltpu.make_async_copy(
            src.at[:, pl.ds(pl.multiple_of(off * cw, cw), cw)], gat.at[ch, z], l_sem.at[ch]
        )

    for c in range(nc):
        own(c, tok, c).start()
    w_copies = [
        pltpu.make_async_copy(wg_hbm, wg, w_sem.at[0]),
        pltpu.make_async_copy(wu_hbm, wu, w_sem.at[1]),
        pltpu.make_async_copy(wd_hbm, wd, w_sem.at[2]),
    ]

    bar = pltpu.get_barrier_semaphore()

    def sig_plane(i, _):
        pl.semaphore_signal(
            bar, inc=1, device_id=peer(lax.rem(col + i, cols), z), device_id_type=MESH
        )
        return 0

    def sig_line(i, _):
        pl.semaphore_signal(
            bar, inc=1, device_id=peer(col, lax.rem(z + i, nz)), device_id_type=MESH
        )
        return 0

    lax.fori_loop(1, cols, sig_plane, 0)
    lax.fori_loop(1, nz, sig_line, 0)
    pl.semaphore_wait(bar, cols + nz - 2)

    def send_meta(i, _):
        pltpu.make_async_remote_copy(
            src_ref=meta, dst_ref=mt.at[z], send_sem=m_send.at[i - 1],
            recv_sem=m_recv.at[i - 1], device_id=peer(col, lax.rem(z + i, nz)),
            device_id_type=MESH,
        ).start()
        return 0

    lax.fori_loop(1, nz, send_meta, 0)

    def ring(ch, s):
        b = along(1 - s)
        pltpu.make_async_remote_copy(
            src_ref=gat.at[ch, b], dst_ref=gat.at[ch, b], send_sem=zg_send.at[ch],
            recv_sem=zg_recv.at[ch, s - 1], device_id=peer(col, zup), device_id_type=MESH,
        ).start()
        if s <= np_:
            b = along(s - 1)
            pltpu.make_async_remote_copy(
                src_ref=gat.at[ch, b], dst_ref=gat.at[ch, b], send_sem=zg_send.at[ch],
                recv_sem=zg_recv.at[ch, nm + s - 1], device_id=peer(col, zdn),
                device_id_type=MESH,
            ).start()

    def ring_wait(ch, s):
        b = along(-s)
        pltpu.make_async_copy(gat.at[ch, b], gat.at[ch, b], zg_recv.at[ch, s - 1]).wait()
        if s <= np_:
            b = along(s)
            pltpu.make_async_copy(
                gat.at[ch, b], gat.at[ch, b], zg_recv.at[ch, nm + s - 1]
            ).wait()

    def ring_first(ch):
        pltpu.make_async_copy(gat.at[ch, z], gat.at[ch, z], l_sem.at[ch]).wait()
        ring(ch, 1)

    def ring_event(ch, s):
        ring_wait(ch, s)
        if s < nm:
            ring(ch, s + 1)

    steps = [(-1 - STRIDE * (nm - s), s) for s in range(nm + 1)]
    early = sorted(
        (t + py * ch, ch, s) for t, s in steps for ch in range(nch) if t + py * ch < 0
    )
    steps = sorted((t % py, -(t // py), s) for t, s in steps)

    def step(ch, s):
        if s == 0:
            ring_first(ch)
        else:
            ring_event(ch, s)

    step(*early[0][1:])
    early = early[1:]
    for c in range(nc):
        own(nc + c, cot, c).start()
    for w in w_copies:
        w.start()

    mt[z] = meta[...]

    def wait_meta(i, _):
        pltpu.make_async_copy(mt.at[z], mt.at[z], m_recv.at[i - 1]).wait()
        return 0

    lax.fori_loop(1, nz, wait_meta, 0)
    exs = cols * el
    before = (
        lax.broadcasted_iota(jnp.int32, (tk, tk), 0) < lax.broadcasted_iota(jnp.int32, (tk, tk), 1)
    ).astype(F32).astype(BF16)
    eye = (
        lax.broadcasted_iota(jnp.int32, (tk, tk), 0) == lax.broadcasted_iota(jnp.int32, (tk, tk), 1)
    ).astype(F32).astype(BF16)
    half = mt.shape[1] // 2

    def route(b, cnt):
        ids = mt[b, 0:half, :].astype(jnp.int32)
        pr = mt[b, half : 2 * half, :]
        lab = lax.broadcasted_iota(jnp.int32, (exs, tk), 0)
        member = jnp.zeros((exs, tk), F32)
        weight = jnp.zeros((exs, tk), F32)
        for k in range(top):
            idk = ids[k : k + 1, :]
            code = (idk // (el * nz)) * el + lax.rem(idk, el)
            code = jnp.where(lax.rem(idk // el, nz) == z, code, -1)
            hit = lab == code
            member = jnp.where(hit, 1.0, member)
            weight = jnp.where(hit, pr[k : k + 1, :], weight)
        rank = jnp.dot(member.astype(BF16), before, preferred_element_type=F32) + cnt
        rank = jnp.where(member > 0.5, rank, -1.0).astype(jnp.int32)
        hi = weight.astype(BF16).astype(F32)
        lo = weight - hi
        at = pl.ds(pl.multiple_of(b * tk, tk), tk)
        for ex in range(exs):
            j = lax.broadcasted_iota(jnp.int32, (sl, tk), 0)
            hit = j == rank[ex : ex + 1, :]
            rows = pl.ds(ex * sl, sl)
            pm[rows, at] = jnp.where(hit, 1.0, 0.0).astype(BF16)
            for i, w in enumerate((hi, lo)):
                stg[nch - 1, ex // el, pl.ds((ex % el) * sl, sl), pl.ds(i * tk, tk)] = (
                    jnp.where(hit, w[ex : ex + 1, :], 0.0).astype(BF16)
                )
        for i in range(2):
            wt[i, at, :] = lax.dot_general(
                eye, stg[nch - 1, :, :, pl.ds(i * tk, tk)].reshape(cols * blk, tk), NT,
                preferred_element_type=F32,
            ).astype(BF16)
        return cnt + jnp.sum(member, axis=1, keepdims=True)

    def route_step(b, cnt):
        for n, (_, ch, s) in enumerate(early):
            @pl.when(b == (n * nz) // len(early))
            def _():
                step(ch, s)
        return route(b, cnt)

    lax.fori_loop(0, nz, route_step, jnp.zeros((exs, 1), F32))
    for w in w_copies:
        w.wait()

    def acc_part(ch, q):
        ys = lax.rem(y - q + py, py)
        rows = pl.ds(ys * px, px)

        @pl.when(q == 0)
        def _():
            pltpu.make_async_copy(rcv.at[ch, col], rcv.at[ch, col], d_self.at[ch]).wait()
            pltpu.make_async_copy(
                rcv.at[ch, pl.ds(0, px - 1)], rcv.at[ch, pl.ds(0, px - 1)], d_recv.at[ch, q]
            ).wait()

        @pl.when(q > 0)
        def _():
            pltpu.make_async_copy(
                rcv.at[ch, pl.ds(0, px)], rcv.at[ch, pl.ds(0, px)], d_recv.at[ch, q]
            ).wait()

        def block(e):
            return rcv[ch, rows, pl.ds(e * sl, sl), :].reshape(px * sl, cw)

        @pl.when(ch < nc)
        def _():
            at = pl.ds(pl.multiple_of(ch * cw, cw), cw)
            for e in range(el):
                v = block(e)
                for h, w in ((0, wg), (1, wu)):
                    r = jnp.dot(v, w[e, at, :], preferred_element_type=F32)
                    gu[h, e, rows] += r.reshape(px, sl, hid)

        @pl.when(ch >= nc)
        def _():
            at = pl.ds(pl.multiple_of((ch - nc) * cw, cw), cw)
            for e in range(el):
                r = lax.dot_general(block(e), wd[e, :, at], NT, preferred_element_type=F32)
                ga[e, rows] += r.reshape(px, sl, hid)

    def wait_d_send(ch):
        pltpu.make_async_copy(
            stg.at[ch, pl.ds(0, cols - 1)], stg.at[ch, pl.ds(0, cols - 1)], d_send.at[ch]
        ).wait()

    gu[...] = jnp.zeros_like(gu)
    ga[...] = jnp.zeros_like(ga)

    def dispatch(i, _):
        ch = i // py
        q = lax.rem(i, py)
        for k, d, s in steps:
            @pl.when((q == k) & (ch + d < nch))
            def _():
                step(ch + d, s)

        @pl.when((q == 0) & (ch >= LAG))
        def _():
            wait_d_send(ch - LAG)

        yd = lax.rem(y + q, py)
        rows = pl.ds(pl.multiple_of(yd * (px * blk), px * blk), px * blk)
        packed = jnp.dot(
            pm[rows, :], gat[ch].reshape(nz * tk, cw), preferred_element_type=F32
        )
        stg[ch, pl.ds(yd * px, px)] = packed.astype(BF16).reshape(px, blk, cw)

        @pl.when(ch >= LAG)
        def _():
            acc_part(ch - LAG, q)

        for ox in range(px):
            d = colat(q, ox)

            def remote():
                pltpu.make_async_remote_copy(
                    src_ref=stg.at[ch, d], dst_ref=rcv.at[ch, col], send_sem=d_send.at[ch],
                    recv_sem=d_recv.at[ch, q], device_id=peer(d, z), device_id_type=MESH,
                ).start()

            if ox == 0:
                @pl.when(q == 0)
                def _():
                    pltpu.make_async_copy(
                        stg.at[ch, col], rcv.at[ch, col], d_self.at[ch]
                    ).start()

                @pl.when(q > 0)
                def _():
                    remote()
            else:
                remote()
        return 0

    lax.fori_loop(0, nch * py, dispatch, 0)

    def wait_zg(ch, _):
        pltpu.make_async_copy(
            gat.at[ch, pl.ds(0, nz - 1)], gat.at[ch, pl.ds(0, nz - 1)], zg_send.at[ch]
        ).wait()
        return 0

    lax.fori_loop(0, nch, wait_zg, 0)
    for zz in (zup, zdn):
        pl.semaphore_signal(credit, inc=1, device_id=peer(col, zz), device_id_type=MESH)

    def forward_act(p, _):
        for e in range(el):
            g = gu[0, e, p]
            act[e, p] = (g * jax.nn.sigmoid(g) * gu[1, e, p]).astype(BF16)
        return 0

    lax.fori_loop(0, cols, forward_act, 0)

    def backward_act(p, _):
        for e in range(el):
            g = gu[0, e, p]
            sig = jax.nn.sigmoid(g)
            d = ga[e, p]
            gg[0, e, p] = (d * gu[1, e, p] * sig * (1.0 + g * (1.0 - sig))).astype(BF16)
            gg[1, e, p] = (d * g * sig).astype(BF16)
        return 0

    def expert_part(r, q):
        rows = pl.ds(lax.rem(y + q, py) * px, px)

        @pl.when(r < nc)
        def _():
            at = pl.ds(pl.multiple_of(r * cw, cw), cw)
            for e in range(el):
                v = act[e, rows].reshape(px * sl, hid)
                o = jnp.dot(v, wd[e, :, at], preferred_element_type=F32)
                rcv[r, rows, pl.ds(e * sl, sl), :] = o.astype(BF16).reshape(px, sl, cw)

        @pl.when(r >= nc)
        def _():
            at = pl.ds(pl.multiple_of((r - nc) * cw, cw), cw)
            for e in range(el):
                o = lax.dot_general(
                    gg[0, e, rows].reshape(px * sl, hid), wg[e, at, :], NT,
                    preferred_element_type=F32,
                ) + lax.dot_general(
                    gg[1, e, rows].reshape(px * sl, hid), wu[e, at, :], NT,
                    preferred_element_type=F32,
                )
                rcv[r, rows, pl.ds(e * sl, sl), :] = o.astype(BF16).reshape(px, sl, cw)

    def combine_part(c, q):
        @pl.when(q == 0)
        def _():
            pltpu.make_async_copy(stg.at[c, col], stg.at[c, col], r_self.at[c]).wait()
            pltpu.make_async_copy(
                stg.at[c, pl.ds(0, px - 1)], stg.at[c, pl.ds(0, px - 1)], r_recv.at[c, q]
            ).wait()

        @pl.when(q > 0)
        def _():
            pltpu.make_async_copy(
                stg.at[c, pl.ds(0, px)], stg.at[c, pl.ds(0, px)], r_recv.at[c, q]
            ).wait()

        ys = lax.rem(y - q + py, py)
        at = pl.ds(pl.multiple_of(ys * (px * blk), px * blk), px * blk)
        v = stg[c, pl.ds(ys * px, px)].reshape(px * blk, cw)
        o = jnp.dot(wt[0, :, at], v, preferred_element_type=F32) + jnp.dot(
            wt[1, :, at], v, preferred_element_type=F32
        )
        o = o.reshape(nz, tk, cw)
        slot = lax.rem(c, slots)

        @pl.when(q == 0)
        def _():
            pt[slot] = o

        @pl.when(q > 0)
        def _():
            pt[slot] += o

    def sum_send(c, s, dn):
        slot = lax.rem(c, slots)
        i = s - 1 if dn else nm + s - 1
        b = along(s - 1 - nm) if dn else along(np_ + 1 - s)
        v = pt[slot, b]
        if s > 1:
            v = v + gat[c, i - 1].astype(F32)
        sb[slot, i] = v.astype(BF16)
        pltpu.make_async_remote_copy(
            src_ref=sb.at[slot, i], dst_ref=gat.at[c, i], send_sem=zr_send.at[c],
            recv_sem=zr_recv.at[c, i], device_id=peer(col, zdn if dn else zup),
            device_id_type=MESH,
        ).start()

    def sum_wait(c, i):
        pltpu.make_async_copy(gat.at[c, i], gat.at[c, i], zr_recv.at[c, i]).wait()

    def out_copy(dst, c, o):
        at = pl.ds(pl.multiple_of(c * cw, cw), cw)
        return pltpu.make_async_copy(ost.at[o], dst.at[:, at], o_sem.at[o])

    def sum_event(c, s):
        if s > 1:
            sum_wait(c, s - 2)
            if s - 1 <= np_:
                sum_wait(c, nm + s - 2)
        if s <= nm:
            sum_send(c, s, True)
        if s <= np_:
            sum_send(c, s, False)
        if s == nm + 1:
            slot = lax.rem(c, slots)
            total = pt[slot, z] + gat[c, nm - 1].astype(F32)
            if np_ > 0:
                total = total + gat[c, nm + np_ - 1].astype(F32)

            o = lax.rem(c, 2)

            @pl.when(c >= 2)
            def _():
                out_copy(o_mix, 0, o).wait()

            ost[o] = total

            @pl.when(c < nc)
            def _():
                out_copy(o_mix, c, o).start()

            @pl.when(c >= nc)
            def _():
                out_copy(o_grad, c - nc, o).start()

            pltpu.make_async_copy(
                gat.at[c, pl.ds(0, nz - 1)], gat.at[c, pl.ds(0, nz - 1)], zr_send.at[c]
            ).wait()

    sums = []
    for s in range(1, nm + 2):
        tick = STRIDE_SUM * (s - 1)
        sums.append((LAG + 1 + tick // py, tick % py, s))
    last = nch + max(d for d, _, _ in sums)

    def give_back(i, _):
        r = i // py
        q = lax.rem(i, py)

        @pl.when((r == LAG + 1) & (q == 0))
        def _():
            pl.semaphore_wait(credit, 2)

        for d, k, s in sorted(sums, key=lambda v: (-v[0], v[1])):
            @pl.when((q == k) & (r >= d) & (r - d < nch))
            def _():
                sum_event(r - d, s)

        @pl.when((q == 0) & (r < LAG))
        def _():
            wait_d_send(nch - LAG + r)

        @pl.when(r < nch)
        def _():
            expert_part(r, q)

        @pl.when((r >= LAG) & (r - LAG < nch))
        def _():
            combine_part(r - LAG, q)

        @pl.when(r < nch)
        def _():
            for ox in range(px):
                d = colat(q, ox)

                def remote():
                    pltpu.make_async_remote_copy(
                        src_ref=rcv.at[r, d], dst_ref=stg.at[r, col], send_sem=r_send.at[r],
                        recv_sem=r_recv.at[r, q], device_id=peer(d, z), device_id_type=MESH,
                    ).start()

                if ox == 0:
                    @pl.when(q == 0)
                    def _():
                        pltpu.make_async_copy(
                            rcv.at[r, col], stg.at[r, col], r_self.at[r]
                        ).start()

                    @pl.when(q > 0)
                    def _():
                        remote()
                else:
                    remote()

        @pl.when(r < LAG)
        def _():
            acc_part(nch - LAG + r, q)

            @pl.when((r == LAG - 1) & (q == py - 1))
            def _():
                lax.fori_loop(0, cols, backward_act, 0)

        return 0

    lax.fori_loop(0, last * py, give_back, 0)

    def finish(ch, _):
        pltpu.make_async_copy(
            rcv.at[ch, pl.ds(0, cols - 1)], rcv.at[ch, pl.ds(0, cols - 1)], r_send.at[ch]
        ).wait()
        return 0

    lax.fori_loop(0, nch, finish, 0)

    for o in range(2):
        out_copy(o_grad, 0, o).wait()

    def finish_meta(i, _):
        pltpu.make_async_copy(mt.at[z], mt.at[z], m_send.at[i - 1]).wait()
        return 0

    lax.fori_loop(1, nz, finish_meta, 0)


def on_device(cfg, tokens, cotangent, expert_ids, probs, gate_weight, up_weight, down_weight):
    py, px, nz, cap, tk, top, dim, hid, el, cw = cfg
    nch = 2 * (dim // cw)
    cols = py * px
    sl = nz * cap
    blk = el * sl
    slots = 1 + -(-(STRIDE_SUM * (nz // 2)) // py)
    half = -(-top // 8) * 8
    pad = ((0, half - top), (0, 0))
    meta = jnp.concatenate(
        [jnp.pad(expert_ids.T.astype(F32), pad), jnp.pad(probs.T, pad)], axis=0
    )
    vm = pl.BlockSpec(memory_space=pltpu.VMEM)
    hbm = pl.BlockSpec(memory_space=pl.ANY)
    dma = pltpu.SemaphoreType.DMA
    return pl.pallas_call(
        functools.partial(moe_kernel, cfg),
        out_shape=(
            jax.ShapeDtypeStruct((tk, dim), F32),
            jax.ShapeDtypeStruct((tk, dim), F32),
        ),
        in_specs=[vm, hbm, hbm, hbm, hbm, hbm],
        out_specs=(hbm, hbm),
        scratch_shapes=[
            pltpu.VMEM((nch, nz, tk, cw), BF16),
            pltpu.VMEM((nch, cols, blk, cw), BF16),
            pltpu.VMEM((nch, cols, blk, cw), BF16),
            pltpu.VMEM(gate_weight.shape, BF16),
            pltpu.VMEM(up_weight.shape, BF16),
            pltpu.VMEM(down_weight.shape, BF16),
            pltpu.VMEM((cols * blk, nz * tk), BF16),
            pltpu.VMEM((2, nz * tk, cols * blk), BF16),
            pltpu.VMEM((2, el, cols, sl, hid), F32),
            pltpu.VMEM((el, cols, sl, hid), F32),
            pltpu.VMEM((el, cols, sl, hid), BF16),
            pltpu.VMEM((2, el, cols, sl, hid), BF16),
            pltpu.VMEM((slots, nz, tk, cw), F32),
            pltpu.VMEM((slots, nz - 1, tk, cw), BF16),
            pltpu.VMEM((2, tk, cw), F32),
            pltpu.VMEM((nz, 2 * half, tk), F32),
            dma((nch,)),
            dma((3,)),
            dma((nz - 1,)),
            dma((nz - 1,)),
            dma((nch,)),
            dma((nch, nz - 1)),
            dma((nch,)),
            dma((nch, py)),
            dma((nch,)),
            dma((nch,)),
            dma((nch, py)),
            dma((nch,)),
            dma((nch,)),
            dma((nch, nz - 1)),
            dma((2,)),
            pltpu.SemaphoreType.REGULAR,
        ],
        compiler_params=pltpu.CompilerParams(
            collective_id=0, has_side_effects=True, vmem_limit_bytes=67043328
        ),
        name="moe",
    )(meta, tokens, cotangent, gate_weight, up_weight, down_weight)


def solution(mesh):
    rows = P(("dp", "expert"), None)
    cubes = P(("dp", "expert"), None, None)

    def body(tokens, cotangent, expert_ids, probs, gate_weight, up_weight, down_weight):
        tk, dim = tokens.shape
        cfg = (PY, PX, Z, CAP, tk, expert_ids.shape[1], dim, gate_weight.shape[2],
               gate_weight.shape[0], min(CHUNK, dim // 2))
        return on_device(
            cfg, tokens, cotangent, expert_ids, probs, gate_weight, up_weight, down_weight
        )

    return jax.shard_map(
        body, mesh=mesh, in_specs=(rows,) * 4 + (cubes,) * 3, out_specs=(rows, rows),
        check_vma=False,
    )
```

```python
import functools

import jax
import jax.numpy as jnp
from jax import lax
from jax.experimental import pallas as pl
from jax.experimental.pallas import tpu as pltpu
from jax.sharding import PartitionSpec as P

MESH = pl.DeviceIdType.MESH
F32 = jnp.float32
BF16 = jnp.bfloat16
NT = (((1,), (1,)), ((), ()))

PY, PX, Z = 4, 4, 8
CAP = 6
CHUNK = 256
STRIDE = 3
STRIDE_SUM = 3
LAG = 4


def moe_kernel(
    cfg, ids_ref, pr_ref, tok, cot, wg_hbm, wu_hbm, wd_hbm, o_mix, o_grad,
    gat, stg, rcv, wg, wu, wd, pm, wt, gu, ga, act, gg, pt, sb, ost, mt,
    l_sem, w_sem, m_send, m_recv, zg_send, zg_recv, d_send, d_recv, d_self,
    r_send, r_recv, r_self, zr_send, zr_recv, o_sem, credit,
):
    py, px, nz, cap, tk, top, dim, hid, el, cw = cfg
    nc = dim // cw
    nch = 2 * nc
    cols = py * px
    sl = nz * cap
    blk = el * sl
    nm = nz // 2
    np_ = nz - 1 - nm
    slots = pt.shape[0]
    me = lax.axis_index("expert")
    z = lax.rem(me, nz)
    col = me // nz
    x = lax.rem(col, px)
    y = col // px

    def peer(c, zz):
        return {"expert": c * nz + zz}

    sense = 1 - 2 * lax.rem(lax.axis_index("dp"), 2)

    def along(n):
        return lax.rem(z + sense * n + 2 * nz, nz)

    zup = along(1)
    zdn = along(-1)

    def colat(oy, ox):
        return lax.rem(y + oy, py) * px + lax.rem(x + ox, px)

    def own(ch, src, off):
        return pltpu.make_async_copy(
            src.at[:, pl.ds(pl.multiple_of(off * cw, cw), cw)], gat.at[ch, z], l_sem.at[ch]
        )

    for c in range(nc):
        own(c, tok, c).start()
    w_copies = [
        pltpu.make_async_copy(wg_hbm, wg, w_sem.at[0]),
        pltpu.make_async_copy(wu_hbm, wu, w_sem.at[1]),
        pltpu.make_async_copy(wd_hbm, wd, w_sem.at[2]),
    ]

    half = mt.shape[1] // 2
    mt[z] = jnp.zeros_like(mt[z])
    mt[z, 0:top, :] = ids_ref[...].astype(F32)
    mt[z, half : half + top, :] = pr_ref[...]

    bar = pltpu.get_barrier_semaphore()

    def sig_plane(i, _):
        pl.semaphore_signal(
            bar, inc=1, device_id=peer(lax.rem(col + i, cols), z), device_id_type=MESH
        )
        return 0

    def sig_line(i, _):
        pl.semaphore_signal(
            bar, inc=1, device_id=peer(col, lax.rem(z + i, nz)), device_id_type=MESH
        )
        return 0

    lax.fori_loop(1, cols, sig_plane, 0)
    lax.fori_loop(1, nz, sig_line, 0)
    pl.semaphore_wait(bar, cols + nz - 2)

    def send_meta(i, _):
        pltpu.make_async_remote_copy(
            src_ref=mt.at[z], dst_ref=mt.at[z], send_sem=m_send.at[i - 1],
            recv_sem=m_recv.at[i - 1], device_id=peer(col, lax.rem(z + i, nz)),
            device_id_type=MESH,
        ).start()
        return 0

    lax.fori_loop(1, nz, send_meta, 0)

    def ring(ch, s):
        b = along(1 - s)
        pltpu.make_async_remote_copy(
            src_ref=gat.at[ch, b], dst_ref=gat.at[ch, b], send_sem=zg_send.at[ch],
            recv_sem=zg_recv.at[ch, s - 1], device_id=peer(col, zup), device_id_type=MESH,
        ).start()
        if s <= np_:
            b = along(s - 1)
            pltpu.make_async_remote_copy(
                src_ref=gat.at[ch, b], dst_ref=gat.at[ch, b], send_sem=zg_send.at[ch],
                recv_sem=zg_recv.at[ch, nm + s - 1], device_id=peer(col, zdn),
                device_id_type=MESH,
            ).start()

    def ring_wait(ch, s):
        b = along(-s)
        pltpu.make_async_copy(gat.at[ch, b], gat.at[ch, b], zg_recv.at[ch, s - 1]).wait()
        if s <= np_:
            b = along(s)
            pltpu.make_async_copy(
                gat.at[ch, b], gat.at[ch, b], zg_recv.at[ch, nm + s - 1]
            ).wait()

    def ring_first(ch, far=False):
        pltpu.make_async_copy(gat.at[ch, z], gat.at[ch, z], l_sem.at[ch]).wait()
        if far:
            pltpu.make_async_remote_copy(
                src_ref=gat.at[ch, z], dst_ref=gat.at[ch, z], send_sem=zg_send.at[ch],
                recv_sem=zg_recv.at[ch, nm - 1], device_id=peer(col, along(nm)),
                device_id_type=MESH,
            ).start()
        ring(ch, 1)

    def ring_event(ch, s, far=False):
        ring_wait(ch, s)
        if s < nm - (1 if far else 0):
            ring(ch, s + 1)

    steps = [(-1 - STRIDE * (nm - s), s) for s in range(nm + 1)]
    early = sorted(
        (t + py * ch, ch, s) for t, s in steps for ch in range(nch) if t + py * ch < 0
    )
    steps = sorted((t % py, -(t // py), s) for t, s in steps)

    def step(ch, s, far=False):
        if s == 0:
            ring_first(ch, far)
        else:
            ring_event(ch, s, far)

    step(*early[0][1:])
    early = early[1:]
    for c in range(nc):
        own(nc + c, cot, c).start()
    for w in w_copies:
        w.start()

    def wait_meta(i, _):
        pltpu.make_async_copy(mt.at[z], mt.at[z], m_recv.at[i - 1]).wait()
        return 0

    lax.fori_loop(1, nz, wait_meta, 0)
    exs = cols * el
    before = (
        lax.broadcasted_iota(jnp.int32, (tk, tk), 0) < lax.broadcasted_iota(jnp.int32, (tk, tk), 1)
    ).astype(F32).astype(BF16)
    eye = (
        lax.broadcasted_iota(jnp.int32, (tk, tk), 0) == lax.broadcasted_iota(jnp.int32, (tk, tk), 1)
    ).astype(F32).astype(BF16)
    def route(b, cnt):
        ids = mt[b, 0:half, :].astype(jnp.int32)
        pr = mt[b, half : 2 * half, :]
        lab = lax.broadcasted_iota(jnp.int32, (exs, tk), 0)
        member = jnp.zeros((exs, tk), F32)
        weight = jnp.zeros((exs, tk), F32)
        for k in range(top):
            idk = ids[k : k + 1, :]
            code = (idk // (el * nz)) * el + lax.rem(idk, el)
            code = jnp.where(lax.rem(idk // el, nz) == z, code, -1)
            hit = lab == code
            member = jnp.where(hit, 1.0, member)
            weight = jnp.where(hit, pr[k : k + 1, :], weight)
        rank = jnp.dot(member.astype(BF16), before, preferred_element_type=F32) + cnt
        rank = jnp.where(member > 0.5, rank, -1.0).astype(jnp.int32)
        hi = weight.astype(BF16).astype(F32)
        lo = weight - hi
        at = pl.ds(pl.multiple_of(b * tk, tk), tk)
        for ex in range(exs):
            j = lax.broadcasted_iota(jnp.int32, (sl, tk), 0)
            hit = j == rank[ex : ex + 1, :]
            rows = pl.ds(ex * sl, sl)
            pm[rows, at] = jnp.where(hit, 1.0, 0.0).astype(BF16)
            for i, w in enumerate((hi, lo)):
                stg[nch - 1, ex // el, pl.ds((ex % el) * sl, sl), pl.ds(i * tk, tk)] = (
                    jnp.where(hit, w[ex : ex + 1, :], 0.0).astype(BF16)
                )
        for i in range(2):
            wt[i, at, :] = lax.dot_general(
                eye, stg[nch - 1, :, :, pl.ds(i * tk, tk)].reshape(cols * blk, tk), NT,
                preferred_element_type=F32,
            ).astype(BF16)
        return cnt + jnp.sum(member, axis=1, keepdims=True)

    def route_step(b, cnt):
        for n, (_, ch, s) in enumerate(early):
            @pl.when(b == (n * nz) // len(early))
            def _():
                step(ch, s)
        return route(b, cnt)

    lax.fori_loop(0, nz, route_step, jnp.zeros((exs, 1), F32))
    for w in w_copies:
        w.wait()

    def acc_part(ch, q):
        ys = lax.rem(y - q + py, py)
        rows = pl.ds(ys * px, px)

        @pl.when(q == 0)
        def _():
            pltpu.make_async_copy(rcv.at[ch, col], rcv.at[ch, col], d_self.at[ch]).wait()
            pltpu.make_async_copy(
                rcv.at[ch, pl.ds(0, px - 1)], rcv.at[ch, pl.ds(0, px - 1)], d_recv.at[ch, q]
            ).wait()

        @pl.when(q > 0)
        def _():
            pltpu.make_async_copy(
                rcv.at[ch, pl.ds(0, px)], rcv.at[ch, pl.ds(0, px)], d_recv.at[ch, q]
            ).wait()

        def block(e):
            return rcv[ch, rows, pl.ds(e * sl, sl), :].reshape(px * sl, cw)

        @pl.when(ch < nc)
        def _():
            at = pl.ds(pl.multiple_of(ch * cw, cw), cw)
            for e in range(el):
                v = block(e)
                for h, w in ((0, wg), (1, wu)):
                    r = jnp.dot(v, w[e, at, :], preferred_element_type=F32)
                    gu[h, e, rows] += r.reshape(px, sl, hid)

        @pl.when(ch >= nc)
        def _():
            at = pl.ds(pl.multiple_of((ch - nc) * cw, cw), cw)
            for e in range(el):
                r = lax.dot_general(block(e), wd[e, :, at], NT, preferred_element_type=F32)
                ga[e, rows] += r.reshape(px, sl, hid)

    def wait_d_send(ch):
        pltpu.make_async_copy(
            stg.at[ch, pl.ds(0, cols - 1)], stg.at[ch, pl.ds(0, cols - 1)], d_send.at[ch]
        ).wait()

    gu[...] = jnp.zeros_like(gu)
    ga[...] = jnp.zeros_like(ga)

    def dispatch(i, _):
        ch = i // py
        q = lax.rem(i, py)
        for k, d, s in steps:
            @pl.when((q == k) & (ch + d < nch))
            def _():
                step(ch + d, s)

        @pl.when((q == 0) & (ch >= LAG))
        def _():
            wait_d_send(ch - LAG)

        yd = lax.rem(y + q, py)
        rows = pl.ds(pl.multiple_of(yd * (px * blk), px * blk), px * blk)
        packed = jnp.dot(
            pm[rows, :], gat[ch].reshape(nz * tk, cw), preferred_element_type=F32
        )
        stg[ch, pl.ds(yd * px, px)] = packed.astype(BF16).reshape(px, blk, cw)

        @pl.when(ch >= LAG)
        def _():
            acc_part(ch - LAG, q)

        for ox in range(px):
            d = colat(q, ox)

            def remote():
                pltpu.make_async_remote_copy(
                    src_ref=stg.at[ch, d], dst_ref=rcv.at[ch, col], send_sem=d_send.at[ch],
                    recv_sem=d_recv.at[ch, q], device_id=peer(d, z), device_id_type=MESH,
                ).start()

            if ox == 0:
                @pl.when(q == 0)
                def _():
                    pltpu.make_async_copy(
                        stg.at[ch, col], rcv.at[ch, col], d_self.at[ch]
                    ).start()

                @pl.when(q > 0)
                def _():
                    remote()
            else:
                remote()
        return 0

    lax.fori_loop(0, nch * py, dispatch, 0)

    def wait_zg(ch, _):
        pltpu.make_async_copy(
            gat.at[ch, pl.ds(0, nz - 1)], gat.at[ch, pl.ds(0, nz - 1)], zg_send.at[ch]
        ).wait()
        return 0

    lax.fori_loop(0, nch, wait_zg, 0)
    for zz in (zup, zdn):
        pl.semaphore_signal(credit, inc=1, device_id=peer(col, zz), device_id_type=MESH)

    def forward_act(p, _):
        for e in range(el):
            g = gu[0, e, p]
            act[e, p] = (g * jax.nn.sigmoid(g) * gu[1, e, p]).astype(BF16)
        return 0

    lax.fori_loop(0, cols, forward_act, 0)

    def backward_act(p, _):
        for e in range(el):
            g = gu[0, e, p]
            sig = jax.nn.sigmoid(g)
            d = ga[e, p]
            gg[0, e, p] = (d * gu[1, e, p] * sig * (1.0 + g * (1.0 - sig))).astype(BF16)
            gg[1, e, p] = (d * g * sig).astype(BF16)
        return 0

    def expert_part(r, q):
        rows = pl.ds(lax.rem(y + q, py) * px, px)

        @pl.when(r < nc)
        def _():
            at = pl.ds(pl.multiple_of(r * cw, cw), cw)
            for e in range(el):
                v = act[e, rows].reshape(px * sl, hid)
                o = jnp.dot(v, wd[e, :, at], preferred_element_type=F32)
                rcv[r, rows, pl.ds(e * sl, sl), :] = o.astype(BF16).reshape(px, sl, cw)

        @pl.when(r >= nc)
        def _():
            at = pl.ds(pl.multiple_of((r - nc) * cw, cw), cw)
            for e in range(el):
                o = lax.dot_general(
                    gg[0, e, rows].reshape(px * sl, hid), wg[e, at, :], NT,
                    preferred_element_type=F32,
                ) + lax.dot_general(
                    gg[1, e, rows].reshape(px * sl, hid), wu[e, at, :], NT,
                    preferred_element_type=F32,
                )
                rcv[r, rows, pl.ds(e * sl, sl), :] = o.astype(BF16).reshape(px, sl, cw)

    def combine_part(c, q):
        @pl.when(q == 0)
        def _():
            pltpu.make_async_copy(stg.at[c, col], stg.at[c, col], r_self.at[c]).wait()
            pltpu.make_async_copy(
                stg.at[c, pl.ds(0, px - 1)], stg.at[c, pl.ds(0, px - 1)], r_recv.at[c, q]
            ).wait()

        @pl.when(q > 0)
        def _():
            pltpu.make_async_copy(
                stg.at[c, pl.ds(0, px)], stg.at[c, pl.ds(0, px)], r_recv.at[c, q]
            ).wait()

        ys = lax.rem(y - q + py, py)
        at = pl.ds(pl.multiple_of(ys * (px * blk), px * blk), px * blk)
        v = stg[c, pl.ds(ys * px, px)].reshape(px * blk, cw)
        o = jnp.dot(wt[0, :, at], v, preferred_element_type=F32) + jnp.dot(
            wt[1, :, at], v, preferred_element_type=F32
        )
        o = o.reshape(nz, tk, cw)
        slot = lax.rem(c, slots)

        @pl.when(q == 0)
        def _():
            pt[slot] = o

        @pl.when(q > 0)
        def _():
            pt[slot] += o

    def sum_send(c, s, dn, fresh=False, far=False):
        slot = lax.rem(c, slots)
        i = s - 1 if dn else nm + s - 1
        b = along(s - 1 - nm) if dn else along(np_ + 1 - s)
        v = pt[slot, b]
        if s > 1 and not fresh:
            v = v + gat[c, i - 1].astype(F32)
        sb[slot, i] = v.astype(BF16)
        pltpu.make_async_remote_copy(
            src_ref=sb.at[slot, i], dst_ref=gat.at[c, i], send_sem=zr_send.at[c],
            recv_sem=zr_recv.at[c, i], device_id=peer(col, along(-nm) if far else zdn if dn else zup),
            device_id_type=MESH,
        ).start()

    def sum_wait(c, i):
        pltpu.make_async_copy(gat.at[c, i], gat.at[c, i], zr_recv.at[c, i]).wait()

    def out_copy(dst, c, o):
        at = pl.ds(pl.multiple_of(c * cw, cw), cw)
        return pltpu.make_async_copy(ost.at[o], dst.at[:, at], o_sem.at[o])

    def finish_sum(c, arrived):
        total = pt[lax.rem(c, slots), z]
        for i in arrived:
            total = total + gat[c, i].astype(F32)
        o = lax.rem(c, 2)

        @pl.when(c >= 2)
        def _():
            out_copy(o_mix, 0, o).wait()

        ost[o] = total

        @pl.when(c < nc)
        def _():
            out_copy(o_mix, c, o).start()

        @pl.when(c >= nc)
        def _():
            out_copy(o_grad, c - nc, o).start()

        pltpu.make_async_copy(
            gat.at[c, pl.ds(0, nz - 1)], gat.at[c, pl.ds(0, nz - 1)], zr_send.at[c]
        ).wait()

    def sum_event(c, s):
        @pl.when(c < nch - 1)
        def _():
            if s > 1:
                sum_wait(c, s - 2)
                if s - 1 <= np_:
                    sum_wait(c, nm + s - 2)
            if s <= nm:
                sum_send(c, s, True)
            if s <= np_:
                sum_send(c, s, False)
            if s == nm + 1:
                finish_sum(c, (nm - 1, nm + np_ - 1))

        @pl.when(c == nch - 1)
        def _():
            if s == 1:
                sum_send(c, 2, True, fresh=True)
                sum_send(c, 1, False)
                sum_send(c, 1, True, far=True)
            elif s < nm:
                sum_wait(c, s - 1)
                sum_send(c, s + 1, True)
                sum_wait(c, nm + s - 2)
                sum_send(c, s, False)
            elif s == nm:
                sum_wait(c, nm - 1)
                sum_wait(c, nm + np_ - 1)
                sum_wait(c, 0)
                finish_sum(c, (nm - 1, nm + np_ - 1, 0))

    sums = []
    for s in range(1, nm + 2):
        tick = STRIDE_SUM * (s - 1)
        sums.append((LAG + 1 + tick // py, tick % py, s))
    last = nch + max(d for d, _, _ in sums)

    def give_back(i, _):
        r = i // py
        q = lax.rem(i, py)

        @pl.when((r == LAG + 1) & (q == 0))
        def _():
            pl.semaphore_wait(credit, 2)

        for d, k, s in sorted(sums, key=lambda v: (-v[0], v[1])):
            @pl.when((q == k) & (r >= d) & (r - d < nch))
            def _():
                sum_event(r - d, s)

        @pl.when((q == 0) & (r < LAG))
        def _():
            wait_d_send(nch - LAG + r)

        @pl.when(r < nch)
        def _():
            expert_part(r, q)

        @pl.when((r >= LAG) & (r - LAG < nch))
        def _():
            combine_part(r - LAG, q)

        @pl.when(r < nch)
        def _():
            for ox in range(px):
                d = colat(q, ox)

                def remote():
                    pltpu.make_async_remote_copy(
                        src_ref=rcv.at[r, d], dst_ref=stg.at[r, col], send_sem=r_send.at[r],
                        recv_sem=r_recv.at[r, q], device_id=peer(d, z), device_id_type=MESH,
                    ).start()

                if ox == 0:
                    @pl.when(q == 0)
                    def _():
                        pltpu.make_async_copy(
                            rcv.at[r, col], stg.at[r, col], r_self.at[r]
                        ).start()

                    @pl.when(q > 0)
                    def _():
                        remote()
                else:
                    remote()

        @pl.when(r < LAG)
        def _():
            acc_part(nch - LAG + r, q)

            @pl.when((r == LAG - 1) & (q == py - 1))
            def _():
                lax.fori_loop(0, cols, backward_act, 0)

        return 0

    lax.fori_loop(0, last * py, give_back, 0)

    def finish(ch, _):
        pltpu.make_async_copy(
            rcv.at[ch, pl.ds(0, cols - 1)], rcv.at[ch, pl.ds(0, cols - 1)], r_send.at[ch]
        ).wait()
        return 0

    lax.fori_loop(0, nch, finish, 0)

    for o in range(2):
        out_copy(o_grad, 0, o).wait()

    def finish_meta(i, _):
        pltpu.make_async_copy(mt.at[z], mt.at[z], m_send.at[i - 1]).wait()
        return 0

    lax.fori_loop(1, nz, finish_meta, 0)


def on_device(cfg, tokens, cotangent, expert_ids, probs, gate_weight, up_weight, down_weight):
    py, px, nz, cap, tk, top, dim, hid, el, cw = cfg
    nch = 2 * (dim // cw)
    cols = py * px
    sl = nz * cap
    blk = el * sl
    slots = 1 + -(-(STRIDE_SUM * (nz // 2)) // py)
    half = -(-top // 8) * 8
    vm = pl.BlockSpec(memory_space=pltpu.VMEM)
    hbm = pl.BlockSpec(memory_space=pl.ANY)
    dma = pltpu.SemaphoreType.DMA
    return pl.pallas_call(
        functools.partial(moe_kernel, cfg),
        out_shape=(
            jax.ShapeDtypeStruct((tk, dim), F32),
            jax.ShapeDtypeStruct((tk, dim), F32),
        ),
        in_specs=[vm, vm, hbm, hbm, hbm, hbm, hbm],
        out_specs=(hbm, hbm),
        scratch_shapes=[
            pltpu.VMEM((nch, nz, tk, cw), BF16),
            pltpu.VMEM((nch, cols, blk, cw), BF16),
            pltpu.VMEM((nch, cols, blk, cw), BF16),
            pltpu.VMEM(gate_weight.shape, BF16),
            pltpu.VMEM(up_weight.shape, BF16),
            pltpu.VMEM(down_weight.shape, BF16),
            pltpu.VMEM((cols * blk, nz * tk), BF16),
            pltpu.VMEM((2, nz * tk, cols * blk), BF16),
            pltpu.VMEM((2, el, cols, sl, hid), F32),
            pltpu.VMEM((el, cols, sl, hid), F32),
            pltpu.VMEM((el, cols, sl, hid), BF16),
            pltpu.VMEM((2, el, cols, sl, hid), BF16),
            pltpu.VMEM((slots, nz, tk, cw), F32),
            pltpu.VMEM((slots, nz - 1, tk, cw), BF16),
            pltpu.VMEM((2, tk, cw), F32),
            pltpu.VMEM((nz, 2 * half, tk), F32),
            dma((nch,)),
            dma((3,)),
            dma((nz - 1,)),
            dma((nz - 1,)),
            dma((nch,)),
            dma((nch, nz - 1)),
            dma((nch,)),
            dma((nch, py)),
            dma((nch,)),
            dma((nch,)),
            dma((nch, py)),
            dma((nch,)),
            dma((nch,)),
            dma((nch, nz - 1)),
            dma((2,)),
            pltpu.SemaphoreType.REGULAR,
        ],
        compiler_params=pltpu.CompilerParams(
            collective_id=0, has_side_effects=True, vmem_limit_bytes=67043328
        ),
        name="moe",
    )(expert_ids.T, probs.T, tokens, cotangent, gate_weight, up_weight, down_weight)


def solution(mesh):
    rows = P(("dp", "expert"), None)
    cubes = P(("dp", "expert"), None, None)

    def body(tokens, cotangent, expert_ids, probs, gate_weight, up_weight, down_weight):
        tk, dim = tokens.shape
        cfg = (PY, PX, Z, CAP, tk, expert_ids.shape[1], dim, gate_weight.shape[2],
               gate_weight.shape[0], min(CHUNK, dim // 2))
        return on_device(
            cfg, tokens, cotangent, expert_ids, probs, gate_weight, up_weight, down_weight
        )

    return jax.shard_map(
        body, mesh=mesh, in_specs=(rows,) * 4 + (cubes,) * 3, out_specs=(rows, rows),
        check_vma=False,
    )
```
